32 devices in a mesh: gx: 4 (over y, core), gy: 8 (over z, x).
Axes of the slice: x: 2, y: 2, z: 4, core: 2. Of those that a mesh axis runs over, the one named last changes fastest.
Arguments:
- perturbation: float32 [5, 16, 512], P(None, 'gx', 'gy'), may hold values from -6 to 6
- mean_velocity: float32 [16, 512], P('gx', 'gy'), may hold values from 0.2 to 0.9
- mean_shear: float32 [16, 512], P('gx', 'gy'), may hold values from -4 to 4
- cotangent: float32 [5, 16, 512], P(None, 'gx', 'gy'), may hold values from -6 to 6
- kernel_in: bfloat16 [64, 135], replicated, may hold values from -0.5 to 0.5
- kernel_mid: bfloat16 [64, 1728], replicated, may hold values from -0.15625 to 0.15625
- kernel_out: bfloat16 [5, 1728], replicated, may hold values from -0.15625 to 0.15625
Outputs:
- advanced: float32 [5, 16, 512], P(None, 'gx', 'gy')
- grad_in: float32 [64, 135], replicated
- grad_mid: float32 [64, 1728], replicated
- grad_out: float32 [5, 1728], replicated
The draws below stay inside these ranges and needn't reach their ends.
All inputs are finite; a program needn't handle non-finite values.
Results may differ from the reference program's by a relative error of at most 0.0065.
Values may be sent and summed in bfloat16 or wider, within the bound.
A program may use at most 64 MiB of HBM per device.

```python
import math
import jax
import jax.numpy as jnp
from jax import lax

NZ = 8
HID = 64
FIELDS = 5
STEPS = 2
NX = 16
NY = 64


def level_of(key, extent, split, least, largest):
    def one(dim, shards_of):
        heights = jax.random.uniform(jax.random.fold_in(jax.random.fold_in(key, 6), dim), (shards_of,), jnp.float32, least / len(split), largest / len(split))
        return jnp.repeat(jnp.exp(heights), extent[dim] // shards_of).reshape((-1,) + (1,) * (len(extent) - dim - 1))

    factor_of = one(*split[0])
    for cut in split[1:]:
        factor_of = factor_of * one(*cut)
    return factor_of


def gaussian(key, shape, width, bound, shards=(), dtype=jnp.bfloat16):
    array = jax.random.normal(key, shape, jnp.float32) * width
    if len(shards) > 0:
        array = level_of(key, shape, shards, -0.22, 0.18) * array
    return jnp.clip(array, min=-bound, max=bound).astype(dtype)


def setup_inputs(seed: int = 0) -> dict:
    splits = jax.random.split(jax.random.key(seed), 8)
    return {
        "perturbation": gaussian(splits[0], (FIELDS, NX, NY * NZ), 1.0, 6.0, ((1, 4), (2, 8)), jnp.float32),
        "mean_velocity": jnp.clip(0.2 + 0.7 * jax.random.uniform(splits[1], (NX, NY * NZ), jnp.float32) ** level_of(splits[1], (NX, NY * NZ), ((0, 4), (1, 8)), -0.2, 0.2), 0.2, 0.9),
        "mean_shear": gaussian(splits[2], (NX, NY * NZ), 1.0, 4.0, ((0, 4), (1, 8)), jnp.float32),
        "cotangent": gaussian(splits[3], (FIELDS, NX, NY * NZ), 1.0, 6.0, ((1, 4), (2, 8)), jnp.float32),
        "kernel_in": gaussian(splits[4], (HID, FIELDS * 27), (FIELDS * 27) ** -0.5, 0.5),
        "kernel_mid": gaussian(splits[5], (HID, HID * 27), (HID * 27) ** -0.5, 0.15625),
        "kernel_out": gaussian(splits[6], (FIELDS, HID * 27), (HID * 27) ** -0.5, 0.15625),
    }


TIME_STEP = 0.25
STENCIL_WEIGHTS = (0.75, -0.15, 1.0 / 60.0)

def wrap_depth(grid_field, margin):
    size_z = grid_field.shape[3]
    return jnp.concatenate([grid_field[:, :, :, size_z - margin:], grid_field, grid_field[:, :, :, :margin]], axis=3)

def difference(padded, direction, margin, length):
    summed = None
    for offset, weight in zip((1, 2, 3), STENCIL_WEIGHTS):
        upper_cells = lax.slice_in_dim(padded, margin + offset, margin + offset + length, axis=direction)
        lower_cells = lax.slice_in_dim(padded, margin - offset, margin - offset + length, axis=direction)
        contrib = weight * (upper_cells - lower_cells)
        summed = contrib if summed is None else summed + contrib
    return summed

def rates_from(padded, margin, velocity, shear_rate):
    size_x = padded.shape[1] - 2 * margin
    size_y = padded.shape[2] - 2 * margin
    interior = padded[:, margin:margin + size_x, margin:margin + size_y]
    slope_x = difference(padded[:, :, margin:margin + size_y], 1, margin, size_x)
    slope_y = difference(padded[:, margin:margin + size_x], 2, margin, size_y)
    slope_z = difference(wrap_depth(interior, 3), 3, 3, interior.shape[3])
    divergence = slope_x[1] + slope_y[2] + slope_z[3]
    return jnp.stack([-velocity * slope_x[0] - divergence, -velocity * slope_x[1] - shear_rate * interior[2] - slope_x[4], -velocity * slope_x[2] - slope_y[4], -velocity * slope_x[3] - slope_z[4], -velocity * slope_x[4] - divergence])

def adjoint_fields(adjoint_in, velocity):
    acoustic = adjoint_in[0] + adjoint_in[4]
    return jnp.stack([velocity * adjoint_in[0], velocity * adjoint_in[1] + acoustic, velocity * adjoint_in[2], velocity * adjoint_in[3], velocity * adjoint_in[4] + adjoint_in[1], acoustic, adjoint_in[2], adjoint_in[3]])

def adjoint_from(padded, margin, adjoint_in, shear_rate):
    size_x = padded.shape[1] - 2 * margin
    size_y = padded.shape[2] - 2 * margin
    interior = padded[:, margin:margin + size_x, margin:margin + size_y]
    slope_x = difference(padded[:5, :, margin:margin + size_y], 1, margin, size_x)
    slope_y = difference(padded[5:, margin:margin + size_x], 2, margin, size_y)
    slope_z = difference(wrap_depth(interior[5:], 3), 3, 3, interior.shape[3])
    return jnp.stack([slope_x[0], slope_x[1], slope_x[2] - shear_rate * adjoint_in[1] + slope_y[0], slope_x[3] + slope_z[0], slope_x[4] + slope_y[1] + slope_z[2]])

def conv_valid(padded, kernel):
    return lax.conv_general_dilated(padded[None], kernel, (1, 1, 1), 'VALID', dimension_numbers=('NCDHW', 'OIDHW', 'NCDHW'), preferred_element_type=jnp.float32)[0]

def flip_kernel(kernel):
    return jnp.transpose(jnp.flip(kernel, (2, 3, 4)), (1, 0, 2, 3, 4))

def kernel_grad(padded, gradient):
    channels = padded.shape[0]
    size_x, size_y, size_z = (gradient.shape[1], gradient.shape[2], gradient.shape[3])
    flat_grad = gradient.reshape(gradient.shape[0], -1)
    pieces = []
    for shift_x in range(3):
        for shift_y in range(3):
            for shift_z in range(3):
                window = padded[:, shift_x:shift_x + size_x, shift_y:shift_y + size_y, shift_z:shift_z + size_z]
                pieces.append(lax.dot_general(flat_grad, window.reshape(channels, -1), (((1,), (1,)), ((), ())), preferred_element_type=jnp.float32))
    stacked = jnp.stack(pieces)
    return jnp.transpose(stacked, (1, 2, 0)).reshape(gradient.shape[0], channels * 27)

def closure_forward(grid_field, kernels, padding_fn):
    kernel_in, kernel_mid, kernel_out = kernels
    padded_in = padding_fn(grid_field.astype(jnp.bfloat16))
    hidden_one = jnp.tanh(conv_valid(padded_in, kernel_in)).astype(jnp.bfloat16)
    padded_one = padding_fn(hidden_one)
    hidden_two = jnp.tanh(conv_valid(padded_one, kernel_mid)).astype(jnp.bfloat16)
    padded_two = padding_fn(hidden_two)
    source = conv_valid(padded_two, kernel_out)
    return (source, (padded_in, hidden_one, padded_one, hidden_two, padded_two))

def closure_backward(saved, source_grad, kernels, need_input, padding_fn):
    kernel_in, kernel_mid, kernel_out = kernels
    padded_in, hidden_one, padded_one, hidden_two, padded_two = saved
    error_out = source_grad.astype(jnp.bfloat16)
    grad_out = kernel_grad(padded_two, error_out)
    back_mid = conv_valid(padding_fn(error_out), flip_kernel(kernel_out)) * (1.0 - jnp.square(hidden_two.astype(jnp.float32)))
    error_mid = back_mid.astype(jnp.bfloat16)
    grad_mid = kernel_grad(padded_one, error_mid)
    back_in = conv_valid(padding_fn(error_mid), flip_kernel(kernel_mid)) * (1.0 - jnp.square(hidden_one.astype(jnp.float32)))
    error_in = back_in.astype(jnp.bfloat16)
    grad_in = kernel_grad(padded_in, error_in)
    state_grad = conv_valid(padding_fn(error_in), flip_kernel(kernel_in)) if need_input else None
    return ((grad_in, grad_mid, grad_out), state_grad)

def retreat(adjoint_in, adjoint_fn):
    into_second = 2.0 / 3.0 * adjoint_in + 2.0 / 3.0 * TIME_STEP * adjoint_fn(adjoint_in)
    direct = 1.0 / 3.0 * adjoint_in
    into_first = 0.25 * into_second + 0.25 * TIME_STEP * adjoint_fn(into_second)
    direct = direct + 0.75 * into_second
    carried = direct + into_first + TIME_STEP * adjoint_fn(into_first)
    source_grad = TIME_STEP * (2.0 / 3.0 * adjoint_in + 0.25 * into_second + into_first)
    return (carried, source_grad)

def zero_pad(grid_field):
    return wrap_depth(jnp.pad(grid_field, ((0, 0), (1, 1), (1, 1), (0, 0))), 1)

def reference(perturbation, mean_velocity, mean_shear, cotangent, kernel_in, kernel_mid, kernel_out):
    channels = perturbation.shape[0]
    hidden = kernel_in.shape[0]
    current = perturbation.reshape(channels, NX, NY, NZ)
    velocity = mean_velocity.reshape(NX, NY, NZ)
    shear_rate = mean_shear.reshape(NX, NY, NZ)
    kernels = (kernel_in.reshape(hidden, channels, 3, 3, 3), kernel_mid.reshape(hidden, hidden, 3, 3, 3), kernel_out.reshape(channels, hidden, 3, 3, 3))

    def section_rates(grid_field):
        return rates_from(jnp.pad(grid_field, ((0, 0), (3, 3), (3, 3), (0, 0))), 3, velocity, shear_rate)

    def adjoint_rates(adjoint_in):
        padded = jnp.pad(adjoint_fields(adjoint_in, velocity), ((0, 0), (3, 3), (3, 3), (0, 0)))
        return adjoint_from(padded, 3, adjoint_in, shear_rate)
    history = []
    for step_index in range(STEPS):
        source = closure_forward(current, kernels, zero_pad)[0]
        history.append(current)
        section_one = current + TIME_STEP * (section_rates(current) + source)
        section_two = 0.75 * current + 0.25 * (section_one + TIME_STEP * (section_rates(section_one) + source))
        current = 1.0 / 3.0 * current + 2.0 / 3.0 * (section_two + TIME_STEP * (section_rates(section_two) + source))
    adjoint_in = cotangent.reshape(channels, NX, NY, NZ) * (1.0 / math.sqrt(NX * NY * NZ))
    totals = None
    for step_index in reversed(range(STEPS)):
        carried, source_grad = retreat(adjoint_in, adjoint_rates)
        saved = closure_forward(history[step_index], kernels, zero_pad)[1]
        kernel_grads, state_grad = closure_backward(saved, source_grad, kernels, step_index > 0, zero_pad)
        totals = kernel_grads if totals is None else tuple((sum_old + sum_new for sum_old, sum_new in zip(totals, kernel_grads)))
        if step_index > 0:
            adjoint_in = carried + state_grad
    return (current.reshape(channels, NX, NY * NZ), totals[0], totals[1], totals[2])
```

```python
import functools
import math

import jax
import jax.numpy as jnp
from jax import lax
from jax.experimental import pallas as pl
from jax.experimental.pallas import tpu as pltpu
from jax.sharding import PartitionSpec as P

NZ = 8
STEPS = 2
LANES = 128

TIME_STEP = 0.25
STENCIL_WEIGHTS = (0.75, -0.15, 1.0 / 60.0)
MESH = pl.DeviceIdType.MESH
WIRE = jnp.float32


def peer(axis, shift, count):
    return {axis: lax.rem(lax.axis_index(axis) + shift, count)}


def greet(count_x, count_y):
    barrier = pltpu.get_barrier_semaphore()
    for axis, count in (("gx", count_x), ("gy", count_y)):
        for shift in range(1, count):
            pl.semaphore_signal(
                barrier, inc=1, device_id=peer(axis, shift, count), device_id_type=MESH
            )
    pl.semaphore_wait(barrier, count_x + count_y - 2)


def spread(axis, count, source, target, send_sem, recv_sem):
    copies = []
    for shift in range(1, count):
        copy = pltpu.make_async_remote_copy(
            src_ref=source(shift),
            dst_ref=target(shift),
            send_sem=send_sem.at[shift - 1],
            recv_sem=recv_sem.at[shift - 1],
            device_id=peer(axis, shift, count),
            device_id_type=MESH,
        )
        copy.start()
        copies.append(copy)
    for copy in copies:
        copy.wait()


def gather_kernel(count_x, count_y, block, full, sx, rx, sy, ry, own_sem):
    index_x = lax.axis_index("gx")
    index_y = lax.axis_index("gy")
    greet(count_x, count_y)
    own = pltpu.make_async_copy(block, full.at[index_y, index_x], own_sem)
    own.start()
    spread("gx", count_x, lambda d: block, lambda d: full.at[index_y, index_x], sx, rx)
    own.wait()
    spread("gy", count_y, lambda d: full.at[index_y], lambda d: full.at[index_y], sy, ry)


def sems(count):
    return pltpu.SemaphoreType.DMA((max(count - 1, 1),))


def gather_fields(fields, collective_id):
    count_x, count_y = lax.axis_size("gx"), lax.axis_size("gy")
    count, size_x, size_yz = fields.shape
    rows = count * size_x * size_yz // LANES
    full = pl.pallas_call(
        functools.partial(gather_kernel, count_x, count_y),
        out_shape=jax.ShapeDtypeStruct((count_y, count_x, rows, LANES), fields.dtype),
        in_specs=[pl.BlockSpec(memory_space=pltpu.VMEM)],
        out_specs=pl.BlockSpec(memory_space=pltpu.VMEM),
        scratch_shapes=[
            sems(count_x),
            sems(count_x),
            sems(count_y),
            sems(count_y),
            pltpu.SemaphoreType.DMA,
        ],
        compiler_params=pltpu.CompilerParams(collective_id=collective_id, has_side_effects=True),
    )(fields.reshape(rows, LANES))
    full = full.reshape(count_y, count_x, count, size_x, size_yz)
    return jnp.transpose(full, (2, 1, 3, 0, 4)).reshape(count, count_x * size_x, count_y * size_yz)


def reduce_kernel(
    count_x, count_y, terms, out, from_x, from_y, part, total,
    s1, r1, s2, r2, s3, r3, s4, r4, own_sem,
):
    index_x = lax.axis_index("gx")
    index_y = lax.axis_index("gy")
    greet(count_x, count_y)
    spread(
        "gx",
        count_x,
        lambda d: terms.at[lax.rem(index_x + d, count_x)],
        lambda d: from_x.at[d - 1],
        s1,
        r1,
    )
    summed = terms[index_x].astype(jnp.float32)
    for shift in range(1, count_x):
        summed = summed + from_x[shift - 1].astype(jnp.float32)
    part[...] = summed.astype(part.dtype)
    spread(
        "gy",
        count_y,
        lambda d: part.at[lax.rem(index_y + d, count_y)],
        lambda d: from_y.at[d - 1],
        s2,
        r2,
    )
    summed = part[index_y].astype(jnp.float32)
    for shift in range(1, count_y):
        summed = summed + from_y[shift - 1].astype(jnp.float32)
    total[...] = summed.astype(total.dtype)
    own = pltpu.make_async_copy(total, out.at[index_x, index_y], own_sem)
    own.start()
    spread("gy", count_y, lambda d: total, lambda d: out.at[index_x, index_y], s3, r3)
    own.wait()
    spread("gx", count_x, lambda d: out.at[index_x], lambda d: out.at[index_x], s4, r4)


def reduce_all(arrays, collective_id):
    count_x, count_y = lax.axis_size("gx"), lax.axis_size("gy")
    flat = jnp.concatenate([a.reshape(-1) for a in arrays]).astype(WIRE)
    size = flat.shape[0]
    unit = count_x * count_y * LANES * 16
    rows = -(-size // unit) * 16
    flat = jnp.pad(flat, (0, rows * LANES * count_x * count_y - size))
    shape = (count_x, count_y, rows, LANES)
    out = pl.pallas_call(
        functools.partial(reduce_kernel, count_x, count_y),
        out_shape=jax.ShapeDtypeStruct(shape, WIRE),
        in_specs=[pl.BlockSpec(memory_space=pltpu.VMEM)],
        out_specs=pl.BlockSpec(memory_space=pltpu.VMEM),
        scratch_shapes=[
            pltpu.VMEM((count_x - 1,) + shape[1:], WIRE),
            pltpu.VMEM((count_y - 1,) + shape[2:], WIRE),
            pltpu.VMEM(shape[1:], WIRE),
            pltpu.VMEM(shape[2:], WIRE),
        ]
        + [sems(c) for c in (count_x, count_x, count_y, count_y) * 1]
        + [sems(c) for c in (count_y, count_y, count_x, count_x)]
        + [pltpu.SemaphoreType.DMA],
        compiler_params=pltpu.CompilerParams(collective_id=collective_id, has_side_effects=True),
    )(flat.reshape(shape))
    out = out.reshape(-1).astype(jnp.float32)
    results, start = [], 0
    for a in arrays:
        results.append(out[start : start + a.size].reshape(a.shape))
        start += a.size
    return results


def slopes(size_x, size_yz):
    row = lax.broadcasted_iota(jnp.int32, (size_x, size_yz), 0)
    lane = lax.broadcasted_iota(jnp.int32, (size_x, size_yz), 1)
    depth = lax.rem(lane, NZ)

    def moved(field, offset, axis):
        return pltpu.roll(field, (-offset) % field.shape[axis], axis)

    def edged(field, axis, position, unit):
        size = field.shape[axis]
        result = None
        for offset, weight in zip((1, 2, 3), STENCIL_WEIGHTS):
            step = offset * unit
            upper = jnp.where(position < size - step, moved(field, step, axis), 0.0)
            lower = jnp.where(position >= step, moved(field, -step, axis), 0.0)
            contrib = weight * (upper - lower)
            result = contrib if result is None else result + contrib
        return result

    def along_x(field):
        return edged(field, 0, row, 1)

    def along_y(field):
        return edged(field, 1, lane, NZ)

    def along_z(field):
        result = None
        for offset, weight in zip((1, 2, 3), STENCIL_WEIGHTS):
            upper = jnp.where(
                depth < NZ - offset, moved(field, offset, 1), moved(field, offset - NZ, 1)
            )
            lower = jnp.where(depth >= offset, moved(field, -offset, 1), moved(field, NZ - offset, 1))
            contrib = weight * (upper - lower)
            result = contrib if result is None else result + contrib
        return result

    return along_x, along_y, along_z


def advance_kernel(now_ref, velocity_ref, shear_ref, source_ref, next_ref):
    fields = range(now_ref.shape[0])
    velocity, shear = velocity_ref[...], shear_ref[...]
    dx, dy, dz = slopes(*velocity.shape)

    def rates(f):
        across = [dx(c) for c in f]
        divergence = across[1] + dy(f[2]) + dz(f[3])
        return (
            -velocity * across[0] - divergence,
            -velocity * across[1] - shear * f[2] - across[4],
            -velocity * across[2] - dy(f[4]),
            -velocity * across[3] - dz(f[4]),
            -velocity * across[4] - divergence,
        )

    now = [now_ref[i] for i in fields]
    rate = rates(now)
    one = [now[i] + TIME_STEP * (rate[i] + source_ref[i]) for i in fields]
    rate = rates(one)
    two = [
        0.75 * now_ref[i] + 0.25 * (one[i] + TIME_STEP * (rate[i] + source_ref[i])) for i in fields
    ]
    rate = rates(two)
    for i in fields:
        next_ref[i] = 1.0 / 3.0 * now_ref[i] + 2.0 / 3.0 * (
            two[i] + TIME_STEP * (rate[i] + source_ref[i])
        )


def retreat_kernel(adjoint_ref, velocity_ref, shear_ref, carried_ref, error_ref):
    fields = range(adjoint_ref.shape[0])
    velocity, shear = velocity_ref[...], shear_ref[...]
    dx, dy, dz = slopes(*velocity.shape)

    def rates(g):
        acoustic = g[0] + g[4]
        return (
            dx(velocity * g[0]),
            dx(velocity * g[1] + acoustic),
            dx(velocity * g[2]) - shear * g[1] + dy(acoustic),
            dx(velocity * g[3]) + dz(acoustic),
            dx(velocity * g[4] + g[1]) + dy(g[2]) + dz(g[3]),
        )

    last = [adjoint_ref[i] for i in fields]
    rate = rates(last)
    second = [2.0 / 3.0 * last[i] + 2.0 / 3.0 * TIME_STEP * rate[i] for i in fields]
    rate = rates(second)
    first = [0.25 * second[i] + 0.25 * TIME_STEP * rate[i] for i in fields]
    for i in fields:
        error_ref[i] = TIME_STEP * (2.0 / 3.0 * adjoint_ref[i] + 0.25 * second[i] + first[i])
    rate = rates(first)
    for i in fields:
        carried_ref[i] = (
            1.0 / 3.0 * adjoint_ref[i] + 0.75 * second[i] + first[i] + TIME_STEP * rate[i]
        )


def whole_call(kernel, outputs, *operands):
    like = jax.ShapeDtypeStruct(operands[0].shape, operands[0].dtype)
    return pl.pallas_call(
        kernel,
        out_shape=[like] * outputs,
        in_specs=[pl.BlockSpec(memory_space=pltpu.VMEM)] * len(operands),
        out_specs=[pl.BlockSpec(memory_space=pltpu.VMEM)] * outputs,
    )(*operands)


def wrap_depth(grid_field, margin):
    size_z = grid_field.shape[3]
    return jnp.concatenate(
        [grid_field[:, :, :, size_z - margin :], grid_field, grid_field[:, :, :, :margin]], axis=3
    )


def conv_valid(padded, kernel):
    return lax.conv_general_dilated(
        padded[None],
        kernel,
        (1, 1, 1),
        "VALID",
        dimension_numbers=("NCDHW", "OIDHW", "NCDHW"),
        preferred_element_type=jnp.float32,
    )[0]


def flip_kernel(kernel):
    return jnp.transpose(jnp.flip(kernel, (2, 3, 4)), (1, 0, 2, 3, 4))


def kernel_grad(steps):
    gradient = steps[0][1]
    out_channels, size_x, size_y, size_z = gradient.shape
    channels = steps[0][0].shape[0]
    wrapped = [wrap_depth(values, 1) for values, _ in steps]
    flat_grad = jnp.concatenate([g.reshape(out_channels, -1) for _, g in steps], axis=1)
    pieces = []
    for a in range(3):
        for b in range(3):
            for c in range(3):
                window = jnp.concatenate(
                    [
                        w[:, a : a + size_x, b : b + size_y, c : c + size_z].reshape(channels, -1)
                        for w in wrapped
                    ],
                    axis=1,
                )
                pieces.append(
                    lax.dot_general(
                        flat_grad,
                        window,
                        (((1,), (1,)), ((), ())),
                        preferred_element_type=jnp.float32,
                    )
                )
    return jnp.stack(pieces)


def kernel_order(stacked):
    return jnp.transpose(stacked, (1, 2, 0)).reshape(stacked.shape[1], -1)


def trim(grid_field, margin, wanted):
    cut = margin - wanted
    if cut == 0:
        return grid_field
    return grid_field[:, cut:-cut, cut:-cut]


def body(perturbation, mean_velocity, mean_shear, cotangent, kernel_in, kernel_mid, kernel_out):
    channels, size_x, size_yz = perturbation.shape
    hidden = kernel_in.shape[0]
    size_y = size_yz // NZ
    index_x, index_y = lax.axis_index("gx"), lax.axis_index("gy")
    grid_x, grid_y = size_x * lax.axis_size("gx"), size_y * lax.axis_size("gy")
    kernels = (
        kernel_in.reshape(hidden, channels, 3, 3, 3),
        kernel_mid.reshape(hidden, hidden, 3, 3, 3),
        kernel_out.reshape(channels, hidden, 3, 3, 3),
    )
    flipped = tuple(flip_kernel(k) for k in kernels)

    def inside(margin):
        at_x = index_x * size_x - margin + jnp.arange(size_x + 2 * margin, dtype=jnp.int32)
        at_y = index_y * size_y - margin + jnp.arange(size_y + 2 * margin, dtype=jnp.int32)
        valid_x = (at_x >= 0) & (at_x < grid_x)
        valid_y = (at_y >= 0) & (at_y < grid_y)
        return (valid_x[:, None] & valid_y[None, :]).astype(jnp.float32)[None, :, :, None]

    def window(whole, margin):
        padded = jnp.pad(
            whole.astype(jnp.bfloat16),
            ((0, 0), (margin, margin), (margin * NZ, margin * NZ)),
        )
        block = lax.dynamic_slice(
            padded,
            (0, index_x * size_x, index_y * size_yz),
            (whole.shape[0], size_x + 2 * margin, size_yz + 2 * margin * NZ),
        )
        return block.reshape(whole.shape[0], size_x + 2 * margin, size_y + 2 * margin, NZ)

    def own(whole):
        return lax.dynamic_slice(
            whole, (0, index_x * size_x, index_y * size_yz), (whole.shape[0], size_x, size_yz)
        )

    def forward(state, margin):
        values = window(state, margin)
        first = (
            jnp.tanh(conv_valid(wrap_depth(values, 1), kernels[0])) * inside(margin - 1)
        ).astype(jnp.bfloat16)
        second = (
            jnp.tanh(conv_valid(wrap_depth(first, 1), kernels[1])) * inside(margin - 2)
        ).astype(jnp.bfloat16)
        source = conv_valid(wrap_depth(trim(second, margin - 2, 1), 1), kernels[2])
        return source.reshape(channels, size_x, size_yz), (values, first, second)

    def backward(error, saved, margin):
        values, first, second = saved
        error_out = window(error, margin - 1)
        slope = (1.0 - jnp.square(second.astype(jnp.float32))) * inside(margin - 2)
        error_mid = (conv_valid(wrap_depth(error_out, 1), flipped[2]) * slope).astype(jnp.bfloat16)
        slope = (
            1.0 - jnp.square(trim(first, margin - 1, margin - 3).astype(jnp.float32))
        ) * inside(margin - 3)
        error_in = (conv_valid(wrap_depth(error_mid, 1), flipped[1]) * slope).astype(jnp.bfloat16)
        pairs = (
            (trim(values, margin, 1), trim(error_in, margin - 3, 0)),
            (trim(first, margin - 1, 1), trim(error_mid, margin - 2, 0)),
            (trim(second, margin - 2, 1), trim(error_out, margin - 1, 0)),
        )
        return pairs, error_in

    everything = gather_fields(
        jnp.concatenate(
            [
                perturbation,
                mean_velocity[None],
                mean_shear[None],
                cotangent * (1.0 / math.sqrt(grid_x * grid_y * NZ)),
            ]
        ),
        0,
    )
    state = everything[:channels]
    velocity, shear = everything[channels], everything[channels + 1]
    adjoint = everything[channels + 2 :]

    stored = []
    for step in range(STEPS):
        margin = 3 if step == 0 else 4
        source, saved = forward(state, margin)
        stored.append((saved, margin))
        state = whole_call(advance_kernel, 1, state, velocity, shear, gather_fields(source, 1))[0]
    gathered = []
    for step in reversed(range(STEPS)):
        carried, error = whole_call(retreat_kernel, 2, adjoint, velocity, shear)
        saved, margin = stored[step]
        pairs, error_in = backward(error, saved, margin)
        gathered.append(pairs)
        if step > 0:
            state_grad = conv_valid(wrap_depth(error_in, 1), flipped[0])
            adjoint = carried + gather_fields(state_grad.reshape(channels, size_x, size_yz), 1)
    grads = [kernel_grad([pairs[i] for pairs in gathered]) for i in range(3)]
    grads = reduce_all(grads, 2)
    return (own(state),) + tuple(kernel_order(g) for g in grads)


def solution(mesh):
    return jax.shard_map(
        body,
        mesh=mesh,
        in_specs=(
            P(None, "gx", "gy"),
            P("gx", "gy"),
            P("gx", "gy"),
            P(None, "gx", "gy"),
            P(),
            P(),
            P(),
        ),
        out_specs=(P(None, "gx", "gy"), P(), P(), P()),
        check_vma=False,
    )
```

```python
import functools
import math

import jax
import jax.numpy as jnp
from jax import lax
from jax.experimental import pallas as pl
from jax.experimental.pallas import tpu as pltpu
from jax.sharding import PartitionSpec as P

NZ = 8
STEPS = 2
LANES = 128

TIME_STEP = 0.25
STENCIL_WEIGHTS = (0.75, -0.15, 1.0 / 60.0)
MESH = pl.DeviceIdType.MESH
WIRE = jnp.bfloat16


def peer(axis, shift, count):
    return {axis: lax.rem(lax.axis_index(axis) + shift, count)}


def greet(count_x, count_y):
    barrier = pltpu.get_barrier_semaphore()
    for axis, count in (("gx", count_x), ("gy", count_y)):
        for shift in range(1, count):
            pl.semaphore_signal(
                barrier, inc=1, device_id=peer(axis, shift, count), device_id_type=MESH
            )
    pl.semaphore_wait(barrier, count_x + count_y - 2)


def spread(axis, count, source, target, send_sem, recv_sem):
    copies = []
    for shift in range(1, count):
        copy = pltpu.make_async_remote_copy(
            src_ref=source(shift),
            dst_ref=target(shift),
            send_sem=send_sem.at[shift - 1],
            recv_sem=recv_sem.at[shift - 1],
            device_id=peer(axis, shift, count),
            device_id_type=MESH,
        )
        copy.start()
        copies.append(copy)
    for copy in copies:
        copy.wait()


def gather_kernel(count_x, count_y, block, full, sx, rx, sy, ry, own_sem):
    index_x = lax.axis_index("gx")
    index_y = lax.axis_index("gy")
    greet(count_x, count_y)
    own = pltpu.make_async_copy(block, full.at[index_x, index_y], own_sem)
    own.start()
    spread("gy", count_y, lambda d: block, lambda d: full.at[index_x, index_y], sy, ry)
    own.wait()
    spread("gx", count_x, lambda d: full.at[index_x], lambda d: full.at[index_x], sx, rx)


def sems(count):
    return pltpu.SemaphoreType.DMA((max(count - 1, 1),))


def gather_fields(fields, collective_id):
    count_x, count_y = lax.axis_size("gx"), lax.axis_size("gy")
    count, size_x, size_yz = fields.shape
    rows = count * size_x * size_yz // LANES
    full = pl.pallas_call(
        functools.partial(gather_kernel, count_x, count_y),
        out_shape=jax.ShapeDtypeStruct((count_x, count_y, rows, LANES), fields.dtype),
        in_specs=[pl.BlockSpec(memory_space=pltpu.VMEM)],
        out_specs=pl.BlockSpec(memory_space=pltpu.VMEM),
        scratch_shapes=[
            sems(count_x),
            sems(count_x),
            sems(count_y),
            sems(count_y),
            pltpu.SemaphoreType.DMA,
        ],
        compiler_params=pltpu.CompilerParams(collective_id=collective_id, has_side_effects=True),
    )(fields.reshape(rows, LANES))
    full = full.reshape(count_x, count_y, count, size_x, size_yz)
    return jnp.transpose(full, (2, 0, 3, 1, 4)).reshape(count, count_x * size_x, count_y * size_yz)


def reduce_kernel(
    count_x, count_y, terms, out, from_x, from_y, part, total,
    s1, r1, s2, r2, s3, r3, s4, r4, own_sem,
):
    index_x = lax.axis_index("gx")
    index_y = lax.axis_index("gy")
    greet(count_x, count_y)
    spread(
        "gx",
        count_x,
        lambda d: terms.at[lax.rem(index_x + d, count_x)],
        lambda d: from_x.at[d - 1],
        s1,
        r1,
    )
    summed = terms[index_x].astype(jnp.float32)
    for shift in range(1, count_x):
        summed = summed + from_x[shift - 1].astype(jnp.float32)
    part[...] = summed.astype(part.dtype)
    spread(
        "gy",
        count_y,
        lambda d: part.at[lax.rem(index_y + d, count_y)],
        lambda d: from_y.at[d - 1],
        s2,
        r2,
    )
    summed = part[index_y].astype(jnp.float32)
    for shift in range(1, count_y):
        summed = summed + from_y[shift - 1].astype(jnp.float32)
    total[...] = summed.astype(total.dtype)
    own = pltpu.make_async_copy(total, out.at[index_x, index_y], own_sem)
    own.start()
    spread("gy", count_y, lambda d: total, lambda d: out.at[index_x, index_y], s3, r3)
    own.wait()
    spread("gx", count_x, lambda d: out.at[index_x], lambda d: out.at[index_x], s4, r4)


def reduce_all(table, collective_id):
    count_x, count_y = lax.axis_size("gx"), lax.axis_size("gy")
    height = table.shape[0]
    rows = table_rows(height) // (count_x * count_y)
    shape = (count_x, count_y, rows, LANES)
    out = pl.pallas_call(
        functools.partial(reduce_kernel, count_x, count_y),
        out_shape=jax.ShapeDtypeStruct(shape, WIRE),
        in_specs=[pl.BlockSpec(memory_space=pltpu.VMEM)],
        out_specs=pl.BlockSpec(memory_space=pltpu.VMEM),
        scratch_shapes=[
            pltpu.VMEM((count_x - 1,) + shape[1:], WIRE),
            pltpu.VMEM((count_y - 1,) + shape[2:], WIRE),
            pltpu.VMEM(shape[1:], WIRE),
            pltpu.VMEM(shape[2:], WIRE),
        ]
        + [sems(c) for c in (count_x, count_x, count_y, count_y) * 1]
        + [sems(c) for c in (count_y, count_y, count_x, count_x)]
        + [pltpu.SemaphoreType.DMA],
        compiler_params=pltpu.CompilerParams(collective_id=collective_id, has_side_effects=True),
    )(table.reshape(shape))
    return out.reshape(height, LANES).astype(jnp.float32)


def table_rows(wanted):
    unit = lax.axis_size("gx") * lax.axis_size("gy") * 16
    return -(-wanted // unit) * unit


def slopes(size_x, size_yz):
    row = lax.broadcasted_iota(jnp.int32, (size_x, size_yz), 0)
    lane = lax.broadcasted_iota(jnp.int32, (size_x, size_yz), 1)
    depth = lax.rem(lane, NZ)

    def moved(field, offset, axis):
        return pltpu.roll(field, (-offset) % field.shape[axis], axis)

    def edged(field, axis, position, unit):
        size = field.shape[axis]
        result = None
        for offset, weight in zip((1, 2, 3), STENCIL_WEIGHTS):
            step = offset * unit
            upper = jnp.where(position < size - step, moved(field, step, axis), 0.0)
            lower = jnp.where(position >= step, moved(field, -step, axis), 0.0)
            contrib = weight * (upper - lower)
            result = contrib if result is None else result + contrib
        return result

    def along_x(field):
        return edged(field, 0, row, 1)

    def along_y(field):
        return edged(field, 1, lane, NZ)

    def along_z(field):
        result = None
        for offset, weight in zip((1, 2, 3), STENCIL_WEIGHTS):
            upper = jnp.where(
                depth < NZ - offset, moved(field, offset, 1), moved(field, offset - NZ, 1)
            )
            lower = jnp.where(depth >= offset, moved(field, -offset, 1), moved(field, NZ - offset, 1))
            contrib = weight * (upper - lower)
            result = contrib if result is None else result + contrib
        return result

    return along_x, along_y, along_z


def advance_kernel(now_ref, velocity_ref, shear_ref, source_ref, next_ref):
    fields = range(now_ref.shape[0])
    velocity, shear = velocity_ref[...], shear_ref[...]
    dx, dy, dz = slopes(*velocity.shape)

    def rates(f):
        across = [dx(c) for c in f]
        divergence = across[1] + dy(f[2]) + dz(f[3])
        return (
            -velocity * across[0] - divergence,
            -velocity * across[1] - shear * f[2] - across[4],
            -velocity * across[2] - dy(f[4]),
            -velocity * across[3] - dz(f[4]),
            -velocity * across[4] - divergence,
        )

    now = [now_ref[i] for i in fields]
    rate = rates(now)
    one = [now[i] + TIME_STEP * (rate[i] + source_ref[i]) for i in fields]
    rate = rates(one)
    two = [
        0.75 * now_ref[i] + 0.25 * (one[i] + TIME_STEP * (rate[i] + source_ref[i])) for i in fields
    ]
    rate = rates(two)
    for i in fields:
        next_ref[i] = 1.0 / 3.0 * now_ref[i] + 2.0 / 3.0 * (
            two[i] + TIME_STEP * (rate[i] + source_ref[i])
        )


def retreat_kernel(adjoint_ref, velocity_ref, shear_ref, carried_ref, error_ref):
    fields = range(adjoint_ref.shape[0])
    velocity, shear = velocity_ref[...], shear_ref[...]
    dx, dy, dz = slopes(*velocity.shape)

    def rates(g):
        acoustic = g[0] + g[4]
        return (
            dx(velocity * g[0]),
            dx(velocity * g[1] + acoustic),
            dx(velocity * g[2]) - shear * g[1] + dy(acoustic),
            dx(velocity * g[3]) + dz(acoustic),
            dx(velocity * g[4] + g[1]) + dy(g[2]) + dz(g[3]),
        )

    last = [adjoint_ref[i] for i in fields]
    rate = rates(last)
    second = [2.0 / 3.0 * last[i] + 2.0 / 3.0 * TIME_STEP * rate[i] for i in fields]
    rate = rates(second)
    first = [0.25 * second[i] + 0.25 * TIME_STEP * rate[i] for i in fields]
    for i in fields:
        error_ref[i] = TIME_STEP * (2.0 / 3.0 * adjoint_ref[i] + 0.25 * second[i] + first[i])
    rate = rates(first)
    for i in fields:
        carried_ref[i] = (
            1.0 / 3.0 * adjoint_ref[i] + 0.75 * second[i] + first[i] + TIME_STEP * rate[i]
        )


def whole_call(kernel, outputs, *operands):
    like = jax.ShapeDtypeStruct(operands[0].shape, operands[0].dtype)
    return pl.pallas_call(
        kernel,
        out_shape=[like] * outputs,
        in_specs=[pl.BlockSpec(memory_space=pltpu.VMEM)] * len(operands),
        out_specs=[pl.BlockSpec(memory_space=pltpu.VMEM)] * outputs,
    )(*operands)


def wrap_depth(grid_field, margin):
    size_z = grid_field.shape[3]
    return jnp.concatenate(
        [grid_field[:, :, :, size_z - margin :], grid_field, grid_field[:, :, :, :margin]], axis=3
    )


def conv_valid(padded, kernel):
    return lax.conv_general_dilated(
        padded[None],
        kernel,
        (1, 1, 1),
        "VALID",
        dimension_numbers=("NCDHW", "OIDHW", "NCDHW"),
        preferred_element_type=jnp.float32,
    )[0]


def flip_kernel(kernel):
    return jnp.transpose(jnp.flip(kernel, (2, 3, 4)), (1, 0, 2, 3, 4))


def up_to(size, unit):
    return -(-size // unit) * unit


def grads_kernel(row_length, *refs):
    *pairs, table, columns = refs
    start = 0
    for index in range(0, len(pairs), 2):
        values, error = pairs[index][...].astype(jnp.float32), pairs[index + 1][...]
        channels, length = values.shape
        depth = lax.rem(lax.broadcasted_iota(jnp.int32, values.shape, 1), NZ)
        above = jnp.where(
            depth < NZ - 1, pltpu.roll(values, length - 1, 1), pltpu.roll(values, NZ - 1, 1)
        )
        below = jnp.where(
            depth >= 1, pltpu.roll(values, 1, 1), pltpu.roll(values, length - NZ + 1, 1)
        )
        place = 0
        for a in range(3):
            for b in range(3):
                shift = (-(a - 1) * row_length - (b - 1) * NZ) % length
                for turned in (below, values, above):
                    moved = pltpu.roll(turned, shift, 1) if shift else turned
                    columns[place : place + channels, :] = moved.astype(columns.dtype)
                    place += channels
        end = up_to(place, LANES)
        if end > place:
            columns[place:end, :] = jnp.zeros((end - place, length), columns.dtype)
        product = lax.dot_general(
            error,
            columns[:end, :],
            (((1,), (1,)), ((), ())),
            preferred_element_type=jnp.float32,
        ).astype(table.dtype)
        height = product.shape[0]
        for j in range(end // LANES):
            table[start : start + height, :] = product[:, j * LANES : (j + 1) * LANES]
            start += height
    if start < table.shape[0]:
        table[start:, :] = jnp.zeros((table.shape[0] - start, LANES), table.dtype)


def kernel_grads(steps, collective_id):
    operands, plans, height, widest = [], [], 0, 0
    for layer in range(len(steps[0])):
        flat_values, flat_error = [], []
        for pairs in steps:
            values, error = pairs[layer]
            padded = jnp.pad(error, ((0, 0), (1, 1), (1, 1), (0, 0)))
            row_length = values.shape[2] * NZ
            for flats, array in ((flat_values, values), (flat_error, padded)):
                flat = array.reshape(array.shape[0], -1)
                more = up_to(flat.shape[0], 16) - flat.shape[0], up_to(flat.shape[1], LANES) - flat.shape[1]
                flats.append(jnp.pad(flat, ((0, more[0]), (0, more[1]))))
        operands += [jnp.concatenate(flat_values, axis=1), jnp.concatenate(flat_error, axis=1)]
        channels, tall = operands[-2].shape[0], operands[-1].shape[0]
        width = up_to(27 * channels, LANES)
        plans.append((height, tall, channels, width, error.shape[0], values.shape[0]))
        height += tall * (width // LANES)
        widest = max(widest, width)
    table = pl.pallas_call(
        functools.partial(grads_kernel, row_length),
        out_shape=jax.ShapeDtypeStruct((table_rows(height), LANES), WIRE),
        in_specs=[pl.BlockSpec(memory_space=pltpu.VMEM)] * len(operands),
        out_specs=pl.BlockSpec(memory_space=pltpu.VMEM),
        scratch_shapes=[pltpu.VMEM((widest, operands[0].shape[1]), jnp.bfloat16)],
    )(*operands)
    table = reduce_all(table, collective_id)
    grads = []
    for start, tall, channels, width, outs, ins in plans:
        block = table[start : start + tall * (width // LANES)].reshape(-1, tall, LANES)
        block = jnp.transpose(block[:, :outs], (1, 0, 2)).reshape(outs, width)
        block = block[:, : 27 * channels].reshape(outs, 27, channels)[:, :, :ins]
        grads.append(jnp.transpose(block, (0, 2, 1)).reshape(outs, ins * 27))
    return tuple(grads)


def trim(grid_field, margin, wanted):
    cut = margin - wanted
    if cut == 0:
        return grid_field
    return grid_field[:, cut:-cut, cut:-cut]


def body(perturbation, mean_velocity, mean_shear, cotangent, kernel_in, kernel_mid, kernel_out):
    channels, size_x, size_yz = perturbation.shape
    hidden = kernel_in.shape[0]
    size_y = size_yz // NZ
    index_x, index_y = lax.axis_index("gx"), lax.axis_index("gy")
    grid_x, grid_y = size_x * lax.axis_size("gx"), size_y * lax.axis_size("gy")
    kernels = (
        kernel_in.reshape(hidden, channels, 3, 3, 3),
        kernel_mid.reshape(hidden, hidden, 3, 3, 3),
        kernel_out.reshape(channels, hidden, 3, 3, 3),
    )
    flipped = tuple(flip_kernel(k) for k in kernels)

    def inside(margin):
        at_x = index_x * size_x - margin + jnp.arange(size_x + 2 * margin, dtype=jnp.int32)
        at_y = index_y * size_y - margin + jnp.arange(size_y + 2 * margin, dtype=jnp.int32)
        valid_x = (at_x >= 0) & (at_x < grid_x)
        valid_y = (at_y >= 0) & (at_y < grid_y)
        return (valid_x[:, None] & valid_y[None, :]).astype(jnp.float32)[None, :, :, None]

    def window(whole, margin):
        padded = jnp.pad(
            whole.astype(jnp.bfloat16),
            ((0, 0), (margin, margin), (margin * NZ, margin * NZ)),
        )
        block = lax.dynamic_slice(
            padded,
            (0, index_x * size_x, index_y * size_yz),
            (whole.shape[0], size_x + 2 * margin, size_yz + 2 * margin * NZ),
        )
        return block.reshape(whole.shape[0], size_x + 2 * margin, size_y + 2 * margin, NZ)

    def own(whole):
        return lax.dynamic_slice(
            whole, (0, index_x * size_x, index_y * size_yz), (whole.shape[0], size_x, size_yz)
        )

    def forward(state, margin):
        values = window(state, margin)
        first = (
            jnp.tanh(conv_valid(wrap_depth(values, 1), kernels[0])) * inside(margin - 1)
        ).astype(jnp.bfloat16)
        second = (
            jnp.tanh(conv_valid(wrap_depth(first, 1), kernels[1])) * inside(margin - 2)
        ).astype(jnp.bfloat16)
        source = conv_valid(wrap_depth(trim(second, margin - 2, 1), 1), kernels[2])
        return source.reshape(channels, size_x, size_yz), (values, first, second)

    def backward(error, saved, margin):
        values, first, second = saved
        error_out = window(error, margin - 1)
        slope = (1.0 - jnp.square(second.astype(jnp.float32))) * inside(margin - 2)
        error_mid = (conv_valid(wrap_depth(error_out, 1), flipped[2]) * slope).astype(jnp.bfloat16)
        slope = (
            1.0 - jnp.square(trim(first, margin - 1, margin - 3).astype(jnp.float32))
        ) * inside(margin - 3)
        error_in = (conv_valid(wrap_depth(error_mid, 1), flipped[1]) * slope).astype(jnp.bfloat16)
        pairs = (
            (trim(values, margin, 1), trim(error_in, margin - 3, 0)),
            (trim(first, margin - 1, 1), trim(error_mid, margin - 2, 0)),
            (trim(second, margin - 2, 1), trim(error_out, margin - 1, 0)),
        )
        return pairs, error_in

    everything = gather_fields(
        jnp.concatenate(
            [
                perturbation,
                mean_velocity[None],
                mean_shear[None],
                cotangent * (1.0 / math.sqrt(grid_x * grid_y * NZ)),
            ]
        ),
        0,
    )
    state = everything[:channels]
    velocity, shear = everything[channels], everything[channels + 1]
    adjoint = everything[channels + 2 :]

    stored = []
    for step in range(STEPS):
        margin = 3 if step == 0 else 4
        source, saved = forward(state, margin)
        stored.append((saved, margin))
        state = whole_call(advance_kernel, 1, state, velocity, shear, gather_fields(source.astype(WIRE), 1).astype(jnp.float32))[0]
    gathered = []
    for step in reversed(range(STEPS)):
        carried, error = whole_call(retreat_kernel, 2, adjoint, velocity, shear)
        saved, margin = stored[step]
        pairs, error_in = backward(error, saved, margin)
        gathered.append(pairs)
        if step > 0:
            state_grad = conv_valid(wrap_depth(error_in, 1), flipped[0])
            adjoint = carried + gather_fields(state_grad.reshape(channels, size_x, size_yz).astype(WIRE), 1).astype(jnp.float32)
    return (own(state),) + kernel_grads(gathered, 2)


def solution(mesh):
    return jax.shard_map(
        body,
        mesh=mesh,
        in_specs=(
            P(None, "gx", "gy"),
            P("gx", "gy"),
            P("gx", "gy"),
            P(None, "gx", "gy"),
            P(),
            P(),
            P(),
        ),
        out_specs=(P(None, "gx", "gy"), P(), P(), P()),
        check_vma=False,
    )
```

```python
import functools
import math

import jax
import jax.numpy as jnp
from jax import lax
from jax.experimental import pallas as pl
from jax.experimental.pallas import tpu as pltpu
from jax.sharding import PartitionSpec as P

NZ = 8
STEPS = 2
LANES = 128

TIME_STEP = 0.25
STENCIL_WEIGHTS = (0.75, -0.15, 1.0 / 60.0)
MESH = pl.DeviceIdType.MESH
WIRE = jnp.bfloat16


def peer(axis, shift, count):
    return {axis: lax.rem(lax.axis_index(axis) + shift, count)}


def greet(count_x, count_y):
    barrier = pltpu.get_barrier_semaphore()
    for axis, count in (("gx", count_x), ("gy", count_y)):
        for shift in range(1, count):
            pl.semaphore_signal(
                barrier, inc=1, device_id=peer(axis, shift, count), device_id_type=MESH
            )
    pl.semaphore_wait(barrier, count_x + count_y - 2)


def spread(axis, count, source, target, send_sem, recv_sem):
    copies = []
    for shift in range(1, count):
        copy = pltpu.make_async_remote_copy(
            src_ref=source(shift),
            dst_ref=target(shift),
            send_sem=send_sem.at[shift - 1],
            recv_sem=recv_sem.at[shift - 1],
            device_id=peer(axis, shift, count),
            device_id_type=MESH,
        )
        copy.start()
        copies.append(copy)
    for copy in copies:
        copy.wait()


def gather_kernel(count_x, count_y, block, full, sx, rx, sy, ry, own_sem):
    index_x = lax.axis_index("gx")
    index_y = lax.axis_index("gy")
    greet(count_x, count_y)
    own = pltpu.make_async_copy(block, full.at[index_x, index_y], own_sem)
    own.start()
    spread("gy", count_y, lambda d: block, lambda d: full.at[index_x, index_y], sy, ry)
    own.wait()
    spread("gx", count_x, lambda d: full.at[index_x], lambda d: full.at[index_x], sx, rx)


def sems(count):
    return pltpu.SemaphoreType.DMA((max(count - 1, 1),))


def gather_fields(fields, collective_id):
    count_x, count_y = lax.axis_size("gx"), lax.axis_size("gy")
    count, size_x, size_yz = fields.shape
    rows = count * size_x * size_yz // LANES
    full = pl.pallas_call(
        functools.partial(gather_kernel, count_x, count_y),
        out_shape=jax.ShapeDtypeStruct((count_x, count_y, rows, LANES), fields.dtype),
        in_specs=[pl.BlockSpec(memory_space=pltpu.VMEM)],
        out_specs=pl.BlockSpec(memory_space=pltpu.VMEM),
        scratch_shapes=[
            sems(count_x),
            sems(count_x),
            sems(count_y),
            sems(count_y),
            pltpu.SemaphoreType.DMA,
        ],
        compiler_params=pltpu.CompilerParams(collective_id=collective_id, has_side_effects=True),
    )(fields.reshape(rows, LANES))
    full = full.reshape(count_x, count_y, count, size_x, size_yz)
    return jnp.transpose(full, (2, 0, 3, 1, 4)).reshape(count, count_x * size_x, count_y * size_yz)


def reduce_kernel(
    count_x, count_y, terms, out, from_x, from_y, part, total,
    s1, r1, s2, r2, s3, r3, s4, r4, own_sem,
):
    index_x = lax.axis_index("gx")
    index_y = lax.axis_index("gy")
    greet(count_x, count_y)
    spread(
        "gx",
        count_x,
        lambda d: terms.at[lax.rem(index_x + d, count_x)],
        lambda d: from_x.at[d - 1],
        s1,
        r1,
    )
    summed = terms[index_x].astype(jnp.float32)
    for shift in range(1, count_x):
        summed = summed + from_x[shift - 1].astype(jnp.float32)
    part[...] = summed.astype(part.dtype)
    spread(
        "gy",
        count_y,
        lambda d: part.at[lax.rem(index_y + d, count_y)],
        lambda d: from_y.at[d - 1],
        s2,
        r2,
    )
    summed = part[index_y].astype(jnp.float32)
    for shift in range(1, count_y):
        summed = summed + from_y[shift - 1].astype(jnp.float32)
    total[...] = summed.astype(total.dtype)
    own = pltpu.make_async_copy(total, out.at[index_x, index_y], own_sem)
    own.start()
    spread("gy", count_y, lambda d: total, lambda d: out.at[index_x, index_y], s3, r3)
    own.wait()
    spread("gx", count_x, lambda d: out.at[index_x], lambda d: out.at[index_x], s4, r4)


def reduce_all(table, collective_id):
    count_x, count_y = lax.axis_size("gx"), lax.axis_size("gy")
    height = table.shape[0]
    rows = table_rows(height) // (count_x * count_y)
    shape = (count_x, count_y, rows, LANES)
    out = pl.pallas_call(
        functools.partial(reduce_kernel, count_x, count_y),
        out_shape=jax.ShapeDtypeStruct(shape, WIRE),
        in_specs=[pl.BlockSpec(memory_space=pltpu.VMEM)],
        out_specs=pl.BlockSpec(memory_space=pltpu.VMEM),
        scratch_shapes=[
            pltpu.VMEM((count_x - 1,) + shape[1:], WIRE),
            pltpu.VMEM((count_y - 1,) + shape[2:], WIRE),
            pltpu.VMEM(shape[1:], WIRE),
            pltpu.VMEM(shape[2:], WIRE),
        ]
        + [sems(c) for c in (count_x, count_x, count_y, count_y) * 1]
        + [sems(c) for c in (count_y, count_y, count_x, count_x)]
        + [pltpu.SemaphoreType.DMA],
        compiler_params=pltpu.CompilerParams(collective_id=collective_id, has_side_effects=True),
    )(table.reshape(shape))
    return out.reshape(height, LANES).astype(jnp.float32)


def table_rows(wanted):
    unit = lax.axis_size("gx") * lax.axis_size("gy") * 16
    return -(-wanted // unit) * unit


def slopes(size_x, size_yz):
    row = lax.broadcasted_iota(jnp.int32, (size_x, size_yz), 0)
    lane = lax.broadcasted_iota(jnp.int32, (size_x, size_yz), 1)
    depth = lax.rem(lane, NZ)

    def moved(field, offset, axis):
        return pltpu.roll(field, (-offset) % field.shape[axis], axis)

    def edged(field, axis, position, unit):
        size = field.shape[axis]
        result = None
        for offset, weight in zip((1, 2, 3), STENCIL_WEIGHTS):
            step = offset * unit
            upper = jnp.where(position < size - step, moved(field, step, axis), 0.0)
            lower = jnp.where(position >= step, moved(field, -step, axis), 0.0)
            contrib = weight * (upper - lower)
            result = contrib if result is None else result + contrib
        return result

    def along_x(field):
        return edged(field, 0, row, 1)

    def along_y(field):
        return edged(field, 1, lane, NZ)

    def along_z(field):
        result = None
        for offset, weight in zip((1, 2, 3), STENCIL_WEIGHTS):
            upper = jnp.where(
                depth < NZ - offset, moved(field, offset, 1), moved(field, offset - NZ, 1)
            )
            lower = jnp.where(depth >= offset, moved(field, -offset, 1), moved(field, NZ - offset, 1))
            contrib = weight * (upper - lower)
            result = contrib if result is None else result + contrib
        return result

    return along_x, along_y, along_z


def advance_kernel(source_at, now_ref, whole_ref, source_ref, next_ref):
    channels = next_ref.shape[0]
    fields = range(channels)
    velocity, shear = whole_ref[channels], whole_ref[channels + 1]
    dx, dy, dz = slopes(*velocity.shape)

    def rates(f):
        across = [dx(c) for c in f]
        divergence = across[1] + dy(f[2]) + dz(f[3])
        return (
            -velocity * across[0] - divergence,
            -velocity * across[1] - shear * f[2] - across[4],
            -velocity * across[2] - dy(f[4]),
            -velocity * across[3] - dz(f[4]),
            -velocity * across[4] - divergence,
        )

    now = [now_ref[i] for i in fields]
    source = [source_ref[source_at + i].astype(jnp.float32) for i in fields]
    rate = rates(now)
    one = [now[i] + TIME_STEP * (rate[i] + source[i]) for i in fields]
    rate = rates(one)
    two = [
        0.75 * now_ref[i] + 0.25 * (one[i] + TIME_STEP * (rate[i] + source[i])) for i in fields
    ]
    rate = rates(two)
    for i in fields:
        next_ref[i] = 1.0 / 3.0 * now_ref[i] + 2.0 / 3.0 * (
            two[i] + TIME_STEP * (rate[i] + source[i])
        )


def retreat_kernel(whole_ref, *refs):
    *later, carried_ref, error_ref = refs
    channels = carried_ref.shape[0]
    fields = range(channels)
    velocity, shear = whole_ref[channels], whole_ref[channels + 1]
    dx, dy, dz = slopes(*velocity.shape)

    def rates(g):
        acoustic = g[0] + g[4]
        return (
            dx(velocity * g[0]),
            dx(velocity * g[1] + acoustic),
            dx(velocity * g[2]) - shear * g[1] + dy(acoustic),
            dx(velocity * g[3]) + dz(acoustic),
            dx(velocity * g[4] + g[1]) + dy(g[2]) + dz(g[3]),
        )

    if later:
        last = [later[0][i] + later[1][i].astype(jnp.float32) for i in fields]
    else:
        last = [whole_ref[channels + 2 + i] for i in fields]
    rate = rates(last)
    second = [2.0 / 3.0 * last[i] + 2.0 / 3.0 * TIME_STEP * rate[i] for i in fields]
    rate = rates(second)
    first = [0.25 * second[i] + 0.25 * TIME_STEP * rate[i] for i in fields]
    for i in fields:
        error_ref[i] = TIME_STEP * (2.0 / 3.0 * last[i] + 0.25 * second[i] + first[i])
    rate = rates(first)
    for i in fields:
        carried_ref[i] = (
            1.0 / 3.0 * last[i] + 0.75 * second[i] + first[i] + TIME_STEP * rate[i]
        )


def whole_call(kernel, channels, outputs, *operands):
    like = jax.ShapeDtypeStruct((channels,) + operands[0].shape[1:], jnp.float32)
    return pl.pallas_call(
        kernel,
        out_shape=[like] * outputs,
        in_specs=[pl.BlockSpec(memory_space=pltpu.VMEM)] * len(operands),
        out_specs=[pl.BlockSpec(memory_space=pltpu.VMEM)] * outputs,
    )(*operands)


def wrap_depth(grid_field, margin):
    size_z = grid_field.shape[3]
    return jnp.concatenate(
        [grid_field[:, :, :, size_z - margin :], grid_field, grid_field[:, :, :, :margin]], axis=3
    )


def conv_valid(padded, kernel):
    return lax.conv_general_dilated(
        padded[None],
        kernel,
        (1, 1, 1),
        "VALID",
        dimension_numbers=("NCDHW", "OIDHW", "NCDHW"),
        preferred_element_type=jnp.float32,
    )[0]


def flip_kernel(kernel):
    return jnp.transpose(jnp.flip(kernel, (2, 3, 4)), (1, 0, 2, 3, 4))


def up_to(size, unit):
    return -(-size // unit) * unit


def grads_kernel(row_length, *refs):
    *pairs, table, columns = refs
    start = 0
    for index in range(0, len(pairs), 2):
        values, error = pairs[index][...].astype(jnp.float32), pairs[index + 1][...]
        channels, length = values.shape
        depth = lax.rem(lax.broadcasted_iota(jnp.int32, values.shape, 1), NZ)
        above = jnp.where(
            depth < NZ - 1, pltpu.roll(values, length - 1, 1), pltpu.roll(values, NZ - 1, 1)
        )
        below = jnp.where(
            depth >= 1, pltpu.roll(values, 1, 1), pltpu.roll(values, length - NZ + 1, 1)
        )
        place = 0
        for a in range(3):
            for b in range(3):
                shift = (-(a - 1) * row_length - (b - 1) * NZ) % length
                for turned in (below, values, above):
                    moved = pltpu.roll(turned, shift, 1) if shift else turned
                    columns[place : place + channels, :] = moved.astype(columns.dtype)
                    place += channels
        end = up_to(place, LANES)
        if end > place:
            columns[place:end, :] = jnp.zeros((end - place, length), columns.dtype)
        product = lax.dot_general(
            error,
            columns[:end, :],
            (((1,), (1,)), ((), ())),
            preferred_element_type=jnp.float32,
        ).astype(table.dtype)
        height = product.shape[0]
        for j in range(end // LANES):
            table[start : start + height, :] = product[:, j * LANES : (j + 1) * LANES]
            start += height
    if start < table.shape[0]:
        table[start:, :] = jnp.zeros((table.shape[0] - start, LANES), table.dtype)


def kernel_grads(steps, collective_id):
    operands, plans, height, widest = [], [], 0, 0
    for layer in range(len(steps[0])):
        flat_values, flat_error = [], []
        for pairs in steps:
            values, error = pairs[layer]
            padded = jnp.pad(error, ((0, 0), (1, 1), (1, 1), (0, 0)))
            row_length = values.shape[2] * NZ
            for flats, array in ((flat_values, values), (flat_error, padded)):
                flat = array.reshape(array.shape[0], -1)
                more = up_to(flat.shape[0], 16) - flat.shape[0], up_to(flat.shape[1], LANES) - flat.shape[1]
                flats.append(jnp.pad(flat, ((0, more[0]), (0, more[1]))))
        operands += [jnp.concatenate(flat_values, axis=1), jnp.concatenate(flat_error, axis=1)]
        channels, tall = operands[-2].shape[0], operands[-1].shape[0]
        width = up_to(27 * channels, LANES)
        plans.append((height, tall, channels, width, error.shape[0], values.shape[0]))
        height += tall * (width // LANES)
        widest = max(widest, width)
    table = pl.pallas_call(
        functools.partial(grads_kernel, row_length),
        out_shape=jax.ShapeDtypeStruct((table_rows(height), LANES), WIRE),
        in_specs=[pl.BlockSpec(memory_space=pltpu.VMEM)] * len(operands),
        out_specs=pl.BlockSpec(memory_space=pltpu.VMEM),
        scratch_shapes=[pltpu.VMEM((widest, operands[0].shape[1]), jnp.bfloat16)],
    )(*operands)
    table = reduce_all(table, collective_id)
    grads = []
    for start, tall, channels, width, outs, ins in plans:
        block = table[start : start + tall * (width // LANES)].reshape(-1, tall, LANES)
        block = jnp.transpose(block[:, :outs], (1, 0, 2)).reshape(outs, width)
        block = block[:, : 27 * channels].reshape(outs, 27, channels)[:, :, :ins]
        grads.append(jnp.transpose(block, (0, 2, 1)).reshape(outs, ins * 27))
    return tuple(grads)


def trim(grid_field, margin, wanted):
    cut = margin - wanted
    if cut == 0:
        return grid_field
    return grid_field[:, cut:-cut, cut:-cut]


def body(perturbation, mean_velocity, mean_shear, cotangent, kernel_in, kernel_mid, kernel_out):
    channels, size_x, size_yz = perturbation.shape
    hidden = kernel_in.shape[0]
    size_y = size_yz // NZ
    index_x, index_y = lax.axis_index("gx"), lax.axis_index("gy")
    grid_x, grid_y = size_x * lax.axis_size("gx"), size_y * lax.axis_size("gy")
    kernels = (
        kernel_in.reshape(hidden, channels, 3, 3, 3),
        kernel_mid.reshape(hidden, hidden, 3, 3, 3),
        kernel_out.reshape(channels, hidden, 3, 3, 3),
    )
    flipped = tuple(flip_kernel(k) for k in kernels)

    def inside(margin):
        at_x = index_x * size_x - margin + jnp.arange(size_x + 2 * margin, dtype=jnp.int32)
        at_y = index_y * size_y - margin + jnp.arange(size_y + 2 * margin, dtype=jnp.int32)
        valid_x = (at_x >= 0) & (at_x < grid_x)
        valid_y = (at_y >= 0) & (at_y < grid_y)
        return (valid_x[:, None] & valid_y[None, :]).astype(jnp.float32)[None, :, :, None]

    def window(whole, margin):
        padded = jnp.pad(
            whole.astype(jnp.bfloat16),
            ((0, 0), (margin, margin), (margin * NZ, margin * NZ)),
        )
        block = lax.dynamic_slice(
            padded,
            (0, index_x * size_x, index_y * size_yz),
            (whole.shape[0], size_x + 2 * margin, size_yz + 2 * margin * NZ),
        )
        return block.reshape(whole.shape[0], size_x + 2 * margin, size_y + 2 * margin, NZ)

    def own(whole):
        return lax.dynamic_slice(
            whole, (0, index_x * size_x, index_y * size_yz), (whole.shape[0], size_x, size_yz)
        )

    def forward(state, margin):
        values = window(state, margin)
        first = (
            jnp.tanh(conv_valid(wrap_depth(values, 1), kernels[0])) * inside(margin - 1)
        ).astype(jnp.bfloat16)
        second = (
            jnp.tanh(conv_valid(wrap_depth(first, 1), kernels[1])) * inside(margin - 2)
        ).astype(jnp.bfloat16)
        source = conv_valid(wrap_depth(trim(second, margin - 2, 1), 1), kernels[2])
        return source.reshape(channels, size_x, size_yz), (values, first, second)

    def backward(error, saved, margin):
        values, first, second = saved
        error_out = window(error, margin - 1)
        slope = (1.0 - jnp.square(second.astype(jnp.float32))) * inside(margin - 2)
        error_mid = (conv_valid(wrap_depth(error_out, 1), flipped[2]) * slope).astype(jnp.bfloat16)
        slope = (
            1.0 - jnp.square(trim(first, margin - 1, margin - 3).astype(jnp.float32))
        ) * inside(margin - 3)
        error_in = (conv_valid(wrap_depth(error_mid, 1), flipped[1]) * slope).astype(jnp.bfloat16)
        pairs = (
            (trim(values, margin, 1), trim(error_in, margin - 3, 0)),
            (trim(first, margin - 1, 1), trim(error_mid, margin - 2, 0)),
            (trim(second, margin - 2, 1), trim(error_out, margin - 1, 0)),
        )
        return pairs, error_in

    everything = gather_fields(
        jnp.concatenate(
            [
                perturbation,
                mean_velocity[None],
                mean_shear[None],
                cotangent * (1.0 / math.sqrt(grid_x * grid_y * NZ)),
            ]
        ),
        0,
    )
    def packed(source):
        return source.reshape(channels, size_x, size_yz).astype(WIRE)

    def advance(now, source, source_at):
        kernel = functools.partial(advance_kernel, source_at)
        return whole_call(kernel, channels, 1, now, everything, source)[0]

    carried, error = whole_call(retreat_kernel, channels, 2, everything)
    state, stored = everything, []
    for step in range(STEPS):
        margin = 3 if step == 0 else 4
        source, saved = forward(state[:channels], margin)
        stored.append((saved, margin))
        if step < STEPS - 1:
            state = advance(state, gather_fields(packed(source), 1), 0)
    gathered, pending = [], packed(source)
    for step in reversed(range(STEPS)):
        saved, margin = stored[step]
        pairs, error_in = backward(error, saved, margin)
        gathered.append(pairs)
        if step > 0:
            sent = packed(conv_valid(wrap_depth(error_in, 1), flipped[0]))
            if pending is not None:
                together = gather_fields(jnp.concatenate([sent, pending]), 3)
                state, pending = advance(state, together, channels), None
            else:
                together = gather_fields(sent, 1)
            carried, error = whole_call(retreat_kernel, channels, 2, everything, carried, together)
    return (own(state),) + kernel_grads(gathered, 2)


def solution(mesh):
    return jax.shard_map(
        body,
        mesh=mesh,
        in_specs=(
            P(None, "gx", "gy"),
            P("gx", "gy"),
            P("gx", "gy"),
            P(None, "gx", "gy"),
            P(),
            P(),
            P(),
        ),
        out_specs=(P(None, "gx", "gy"), P(), P(), P()),
        check_vma=False,
    )
```

```python
import functools
import math

import jax
import jax.numpy as jnp
from jax import lax
from jax.experimental import pallas as pl
from jax.experimental.pallas import tpu as pltpu
from jax.sharding import PartitionSpec as P

NZ = 8
STEPS = 2
LANES = 128

TIME_STEP = 0.25
STENCIL_WEIGHTS = (0.75, -0.15, 1.0 / 60.0)
MESH = pl.DeviceIdType.MESH
WIRE = jnp.bfloat16


def peer(axis, shift, count):
    return {axis: lax.rem(lax.axis_index(axis) + shift, count)}


def greet(count_x, count_y):
    barrier = pltpu.get_barrier_semaphore()
    for axis, count in (("gx", count_x), ("gy", count_y)):
        for shift in range(1, count):
            pl.semaphore_signal(
                barrier, inc=1, device_id=peer(axis, shift, count), device_id_type=MESH
            )
    pl.semaphore_wait(barrier, count_x + count_y - 2)


def spread(axis, count, source, target, send_sem, recv_sem):
    copies = []
    for shift in range(1, count):
        copy = pltpu.make_async_remote_copy(
            src_ref=source(shift),
            dst_ref=target(shift),
            send_sem=send_sem.at[shift - 1],
            recv_sem=recv_sem.at[shift - 1],
            device_id=peer(axis, shift, count),
            device_id_type=MESH,
        )
        copy.start()
        copies.append(copy)
    for copy in copies:
        copy.wait()


def gather_kernel(count_x, count_y, block, full, sx, rx, sy, ry, own_sem):
    index_x = lax.axis_index("gx")
    index_y = lax.axis_index("gy")
    greet(count_x, count_y)
    own = pltpu.make_async_copy(block, full.at[index_x, index_y], own_sem)
    own.start()
    spread("gy", count_y, lambda d: block, lambda d: full.at[index_x, index_y], sy, ry)
    own.wait()
    spread("gx", count_x, lambda d: full.at[index_x], lambda d: full.at[index_x], sx, rx)


def sems(count):
    return pltpu.SemaphoreType.DMA((max(count - 1, 1),))


def gather_fields(fields, collective_id):
    count_x, count_y = lax.axis_size("gx"), lax.axis_size("gy")
    count, size_x, size_yz = fields.shape
    rows = count * size_x * size_yz // LANES
    full = pl.pallas_call(
        functools.partial(gather_kernel, count_x, count_y),
        out_shape=jax.ShapeDtypeStruct((count_x, count_y, rows, LANES), fields.dtype),
        in_specs=[pl.BlockSpec(memory_space=pltpu.VMEM)],
        out_specs=pl.BlockSpec(memory_space=pltpu.VMEM),
        scratch_shapes=[
            sems(count_x),
            sems(count_x),
            sems(count_y),
            sems(count_y),
            pltpu.SemaphoreType.DMA,
        ],
        compiler_params=pltpu.CompilerParams(collective_id=collective_id, has_side_effects=True),
    )(fields.reshape(rows, LANES))
    full = full.reshape(count_x, count_y, count, size_x, size_yz)
    return jnp.transpose(full, (2, 0, 3, 1, 4)).reshape(count, count_x * size_x, count_y * size_yz)


def reduce_kernel(
    count_x, count_y, terms, out, from_x, from_y, part, total,
    s1, r1, s2, r2, s3, r3, s4, r4, own_sem,
):
    index_x = lax.axis_index("gx")
    index_y = lax.axis_index("gy")
    greet(count_x, count_y)
    spread(
        "gx",
        count_x,
        lambda d: terms.at[lax.rem(index_x + d, count_x)],
        lambda d: from_x.at[d - 1],
        s1,
        r1,
    )
    summed = terms[index_x].astype(jnp.float32)
    for shift in range(1, count_x):
        summed = summed + from_x[shift - 1].astype(jnp.float32)
    part[...] = summed.astype(part.dtype)
    spread(
        "gy",
        count_y,
        lambda d: part.at[lax.rem(index_y + d, count_y)],
        lambda d: from_y.at[d - 1],
        s2,
        r2,
    )
    summed = part[index_y].astype(jnp.float32)
    for shift in range(1, count_y):
        summed = summed + from_y[shift - 1].astype(jnp.float32)
    total[...] = summed.astype(total.dtype)
    own = pltpu.make_async_copy(total, out.at[index_x, index_y], own_sem)
    own.start()
    spread("gy", count_y, lambda d: total, lambda d: out.at[index_x, index_y], s3, r3)
    own.wait()
    spread("gx", count_x, lambda d: out.at[index_x], lambda d: out.at[index_x], s4, r4)


def reduce_all(table, collective_id):
    count_x, count_y = lax.axis_size("gx"), lax.axis_size("gy")
    height = table.shape[0]
    rows = table_rows(height) // (count_x * count_y)
    shape = (count_x, count_y, rows, LANES)
    out = pl.pallas_call(
        functools.partial(reduce_kernel, count_x, count_y),
        out_shape=jax.ShapeDtypeStruct(shape, WIRE),
        in_specs=[pl.BlockSpec(memory_space=pltpu.VMEM)],
        out_specs=pl.BlockSpec(memory_space=pltpu.VMEM),
        scratch_shapes=[
            pltpu.VMEM((count_x - 1,) + shape[1:], WIRE),
            pltpu.VMEM((count_y - 1,) + shape[2:], WIRE),
            pltpu.VMEM(shape[1:], WIRE),
            pltpu.VMEM(shape[2:], WIRE),
        ]
        + [sems(c) for c in (count_x, count_x, count_y, count_y) * 1]
        + [sems(c) for c in (count_y, count_y, count_x, count_x)]
        + [pltpu.SemaphoreType.DMA],
        compiler_params=pltpu.CompilerParams(collective_id=collective_id, has_side_effects=True),
    )(table.reshape(shape))
    return out.reshape(height, LANES).astype(jnp.float32)


def table_rows(wanted):
    unit = lax.axis_size("gx") * lax.axis_size("gy") * 8
    return -(-wanted // unit) * unit


def slopes(size_x, size_yz):
    row = lax.broadcasted_iota(jnp.int32, (size_x, size_yz), 0)
    lane = lax.broadcasted_iota(jnp.int32, (size_x, size_yz), 1)
    depth = lax.rem(lane, NZ)

    def moved(field, offset, axis):
        return pltpu.roll(field, (-offset) % field.shape[axis], axis)

    def edged(field, axis, position, unit):
        size = field.shape[axis]
        result = None
        for offset, weight in zip((1, 2, 3), STENCIL_WEIGHTS):
            step = offset * unit
            upper = jnp.where(position < size - step, moved(field, step, axis), 0.0)
            lower = jnp.where(position >= step, moved(field, -step, axis), 0.0)
            contrib = weight * (upper - lower)
            result = contrib if result is None else result + contrib
        return result

    def along_x(field):
        return edged(field, 0, row, 1)

    def along_y(field):
        return edged(field, 1, lane, NZ)

    def along_z(field):
        result = None
        for offset, weight in zip((1, 2, 3), STENCIL_WEIGHTS):
            upper = jnp.where(
                depth < NZ - offset, moved(field, offset, 1), moved(field, offset - NZ, 1)
            )
            lower = jnp.where(depth >= offset, moved(field, -offset, 1), moved(field, NZ - offset, 1))
            contrib = weight * (upper - lower)
            result = contrib if result is None else result + contrib
        return result

    return along_x, along_y, along_z


def advance_kernel(source_at, now_ref, whole_ref, source_ref, next_ref):
    channels = next_ref.shape[0]
    fields = range(channels)
    velocity, shear = whole_ref[channels], whole_ref[channels + 1]
    dx, dy, dz = slopes(*velocity.shape)

    def rates(f):
        across = [dx(c) for c in f]
        divergence = across[1] + dy(f[2]) + dz(f[3])
        return (
            -velocity * across[0] - divergence,
            -velocity * across[1] - shear * f[2] - across[4],
            -velocity * across[2] - dy(f[4]),
            -velocity * across[3] - dz(f[4]),
            -velocity * across[4] - divergence,
        )

    now = [now_ref[i] for i in fields]
    source = [source_ref[source_at + i].astype(jnp.float32) for i in fields]
    rate = rates(now)
    one = [now[i] + TIME_STEP * (rate[i] + source[i]) for i in fields]
    rate = rates(one)
    two = [
        0.75 * now_ref[i] + 0.25 * (one[i] + TIME_STEP * (rate[i] + source[i])) for i in fields
    ]
    rate = rates(two)
    for i in fields:
        next_ref[i] = 1.0 / 3.0 * now_ref[i] + 2.0 / 3.0 * (
            two[i] + TIME_STEP * (rate[i] + source[i])
        )


def retreat_kernel(whole_ref, *refs):
    *later, carried_ref, error_ref = refs
    channels = carried_ref.shape[0]
    fields = range(channels)
    velocity, shear = whole_ref[channels], whole_ref[channels + 1]
    dx, dy, dz = slopes(*velocity.shape)

    def rates(g):
        acoustic = g[0] + g[4]
        return (
            dx(velocity * g[0]),
            dx(velocity * g[1] + acoustic),
            dx(velocity * g[2]) - shear * g[1] + dy(acoustic),
            dx(velocity * g[3]) + dz(acoustic),
            dx(velocity * g[4] + g[1]) + dy(g[2]) + dz(g[3]),
        )

    if later:
        last = [later[0][i] + later[1][i].astype(jnp.float32) for i in fields]
    else:
        last = [whole_ref[channels + 2 + i] for i in fields]
    rate = rates(last)
    second = [2.0 / 3.0 * last[i] + 2.0 / 3.0 * TIME_STEP * rate[i] for i in fields]
    rate = rates(second)
    first = [0.25 * second[i] + 0.25 * TIME_STEP * rate[i] for i in fields]
    for i in fields:
        error_ref[i] = TIME_STEP * (2.0 / 3.0 * last[i] + 0.25 * second[i] + first[i])
    rate = rates(first)
    for i in fields:
        carried_ref[i] = (
            1.0 / 3.0 * last[i] + 0.75 * second[i] + first[i] + TIME_STEP * rate[i]
        )


def whole_call(kernel, channels, outputs, *operands):
    like = jax.ShapeDtypeStruct((channels,) + operands[0].shape[1:], jnp.float32)
    return pl.pallas_call(
        kernel,
        out_shape=[like] * outputs,
        in_specs=[pl.BlockSpec(memory_space=pltpu.VMEM)] * len(operands),
        out_specs=[pl.BlockSpec(memory_space=pltpu.VMEM)] * outputs,
    )(*operands)


def wrap_depth(grid_field, margin):
    size_z = grid_field.shape[3]
    return jnp.concatenate(
        [grid_field[:, :, :, size_z - margin :], grid_field, grid_field[:, :, :, :margin]], axis=3
    )


def conv_valid(padded, kernel):
    return lax.conv_general_dilated(
        padded[None],
        kernel,
        (1, 1, 1),
        "VALID",
        dimension_numbers=("NCDHW", "OIDHW", "NCDHW"),
        preferred_element_type=jnp.float32,
    )[0]


def flip_kernel(kernel):
    return jnp.transpose(jnp.flip(kernel, (2, 3, 4)), (1, 0, 2, 3, 4))


def up_to(size, unit):
    return -(-size // unit) * unit


def grads_kernel(row_length, *refs):
    *pairs, table, columns = refs
    start = 0
    for index in range(0, len(pairs), 2):
        values, error = pairs[index][...].astype(jnp.float32), pairs[index + 1][...]
        channels, length = values.shape
        depth = lax.rem(lax.broadcasted_iota(jnp.int32, values.shape, 1), NZ)
        above = jnp.where(
            depth < NZ - 1, pltpu.roll(values, length - 1, 1), pltpu.roll(values, NZ - 1, 1)
        )
        below = jnp.where(
            depth >= 1, pltpu.roll(values, 1, 1), pltpu.roll(values, length - NZ + 1, 1)
        )
        place = 0
        for a in range(3):
            for b in range(3):
                shift = (-(a - 1) * row_length - (b - 1) * NZ) % length
                for turned in (below, values, above):
                    moved = pltpu.roll(turned, shift, 1) if shift else turned
                    columns[place : place + channels, :] = moved.astype(columns.dtype)
                    place += channels
        end = up_to(place, LANES)
        if end > place:
            columns[place:end, :] = jnp.zeros((end - place, length), columns.dtype)
        product = lax.dot_general(
            error,
            columns[:end, :],
            (((1,), (1,)), ((), ())),
            preferred_element_type=jnp.float32,
        ).astype(table.dtype)
        height = product.shape[0]
        for j in range(end // LANES):
            table[start : start + height, :] = product[:, j * LANES : (j + 1) * LANES]
            start += height
    if start < table.shape[0]:
        table[start:, :] = jnp.zeros((table.shape[0] - start, LANES), table.dtype)


def kernel_grads(steps, collective_id):
    operands, plans, height, widest = [], [], 0, 0
    for layer in range(len(steps[0])):
        flat_values, flat_error = [], []
        for pairs in steps:
            values, error = pairs[layer]
            padded = jnp.pad(error, ((0, 0), (1, 1), (1, 1), (0, 0)))
            row_length = values.shape[2] * NZ
            for flats, array in ((flat_values, values), (flat_error, padded)):
                flat = array.reshape(array.shape[0], -1)
                more = up_to(flat.shape[0], 16) - flat.shape[0], up_to(flat.shape[1], LANES) - flat.shape[1]
                flats.append(jnp.pad(flat, ((0, more[0]), (0, more[1]))))
        operands += [jnp.concatenate(flat_values, axis=1), jnp.concatenate(flat_error, axis=1)]
        channels, tall = operands[-2].shape[0], operands[-1].shape[0]
        width = up_to(27 * channels, LANES)
        plans.append((height, tall, channels, width, error.shape[0], values.shape[0]))
        height += tall * (width // LANES)
        widest = max(widest, width)
    table = pl.pallas_call(
        functools.partial(grads_kernel, row_length),
        out_shape=jax.ShapeDtypeStruct((table_rows(height), LANES), WIRE),
        in_specs=[pl.BlockSpec(memory_space=pltpu.VMEM)] * len(operands),
        out_specs=pl.BlockSpec(memory_space=pltpu.VMEM),
        scratch_shapes=[pltpu.VMEM((widest, operands[0].shape[1]), jnp.bfloat16)],
    )(*operands)
    table = reduce_all(table, collective_id)
    grads = []
    for start, tall, channels, width, outs, ins in plans:
        block = table[start : start + tall * (width // LANES)].reshape(-1, tall, LANES)
        block = jnp.transpose(block[:, :outs], (1, 0, 2)).reshape(outs, width)
        block = block[:, : 27 * channels].reshape(outs, 27, channels)[:, :, :ins]
        grads.append(jnp.transpose(block, (0, 2, 1)).reshape(outs, ins * 27))
    return tuple(grads)


def trim(grid_field, margin, wanted):
    cut = margin - wanted
    if cut == 0:
        return grid_field
    return grid_field[:, cut:-cut, cut:-cut]


def body(perturbation, mean_velocity, mean_shear, cotangent, kernel_in, kernel_mid, kernel_out):
    channels, size_x, size_yz = perturbation.shape
    hidden = kernel_in.shape[0]
    size_y = size_yz // NZ
    index_x, index_y = lax.axis_index("gx"), lax.axis_index("gy")
    grid_x, grid_y = size_x * lax.axis_size("gx"), size_y * lax.axis_size("gy")
    kernels = (
        kernel_in.reshape(hidden, channels, 3, 3, 3),
        kernel_mid.reshape(hidden, hidden, 3, 3, 3),
        kernel_out.reshape(channels, hidden, 3, 3, 3),
    )
    flipped = tuple(flip_kernel(k) for k in kernels)

    def inside(margin):
        at_x = index_x * size_x - margin + jnp.arange(size_x + 2 * margin, dtype=jnp.int32)
        at_y = index_y * size_y - margin + jnp.arange(size_y + 2 * margin, dtype=jnp.int32)
        valid_x = (at_x >= 0) & (at_x < grid_x)
        valid_y = (at_y >= 0) & (at_y < grid_y)
        return (valid_x[:, None] & valid_y[None, :]).astype(jnp.float32)[None, :, :, None]

    def window(whole, margin):
        padded = jnp.pad(
            whole.astype(jnp.bfloat16),
            ((0, 0), (margin, margin), (margin * NZ, margin * NZ)),
        )
        block = lax.dynamic_slice(
            padded,
            (0, index_x * size_x, index_y * size_yz),
            (whole.shape[0], size_x + 2 * margin, size_yz + 2 * margin * NZ),
        )
        return block.reshape(whole.shape[0], size_x + 2 * margin, size_y + 2 * margin, NZ)

    def own(whole):
        return lax.dynamic_slice(
            whole, (0, index_x * size_x, index_y * size_yz), (whole.shape[0], size_x, size_yz)
        )

    def forward(state, margin):
        values = window(state, margin)
        first = (
            jnp.tanh(conv_valid(wrap_depth(values, 1), kernels[0])) * inside(margin - 1)
        ).astype(jnp.bfloat16)
        second = (
            jnp.tanh(conv_valid(wrap_depth(first, 1), kernels[1])) * inside(margin - 2)
        ).astype(jnp.bfloat16)
        source = conv_valid(wrap_depth(trim(second, margin - 2, 1), 1), kernels[2])
        return source.reshape(channels, size_x, size_yz), (values, first, second)

    def backward(error, saved, margin):
        values, first, second = saved
        error_out = window(error, margin - 1)
        slope = (1.0 - jnp.square(second.astype(jnp.float32))) * inside(margin - 2)
        error_mid = (conv_valid(wrap_depth(error_out, 1), flipped[2]) * slope).astype(jnp.bfloat16)
        slope = (
            1.0 - jnp.square(trim(first, margin - 1, margin - 3).astype(jnp.float32))
        ) * inside(margin - 3)
        error_in = (conv_valid(wrap_depth(error_mid, 1), flipped[1]) * slope).astype(jnp.bfloat16)
        pairs = (
            (trim(values, margin, 1), trim(error_in, margin - 3, 0)),
            (trim(first, margin - 1, 1), trim(error_mid, margin - 2, 0)),
            (trim(second, margin - 2, 1), trim(error_out, margin - 1, 0)),
        )
        return pairs, error_in

    everything = gather_fields(
        jnp.concatenate(
            [
                perturbation,
                mean_velocity[None],
                mean_shear[None],
                cotangent * (1.0 / math.sqrt(grid_x * grid_y * NZ)),
            ]
        ),
        0,
    )
    def packed(source):
        return source.reshape(channels, size_x, size_yz).astype(WIRE)

    def advance(now, source, source_at):
        kernel = functools.partial(advance_kernel, source_at)
        return whole_call(kernel, channels, 1, now, everything, source)[0]

    carried, error = whole_call(retreat_kernel, channels, 2, everything)
    state, stored = everything, []
    for step in range(STEPS):
        margin = 3 if step == 0 else 4
        source, saved = forward(state[:channels], margin)
        stored.append((saved, margin))
        if step < STEPS - 1:
            state = advance(state, gather_fields(packed(source), 1), 0)
    gathered, pending = [], packed(source)
    for step in reversed(range(STEPS)):
        saved, margin = stored[step]
        pairs, error_in = backward(error, saved, margin)
        gathered.append(pairs)
        if step > 0:
            sent = packed(conv_valid(wrap_depth(error_in, 1), flipped[0]))
            if pending is not None:
                together = gather_fields(jnp.concatenate([sent, pending]), 3)
                state, pending = advance(state, together, channels), None
            else:
                together = gather_fields(sent, 1)
            carried, error = whole_call(retreat_kernel, channels, 2, everything, carried, together)
    return (own(state),) + kernel_grads(gathered, 2)


def solution(mesh):
    return jax.shard_map(
        body,
        mesh=mesh,
        in_specs=(
            P(None, "gx", "gy"),
            P("gx", "gy"),
            P("gx", "gy"),
            P(None, "gx", "gy"),
            P(),
            P(),
            P(),
        ),
        out_specs=(P(None, "gx", "gy"), P(), P(), P()),
        check_vma=False,
    )
```
